32 devices in a mesh: group: 1, expert: 16 (over z, y, x), dp: 2 (over core).
Axes of the slice: x: 2, y: 2, z: 4, core: 2. Of those that a mesh axis runs over, the one named last changes fastest.
Arguments:
- tokens: bfloat16 [2048, 4096], P(('group', 'expert', 'dp')), may hold values from -6 to 6
- queries: bfloat16 [2048, 4096], P(('group', 'expert', 'dp')), may hold values from -6 to 6
- keys_local: bfloat16 [2048, 256], P(('group', 'expert', 'dp')), may hold values from -6 to 6
- values_local: bfloat16 [2048, 256], P(('group', 'expert', 'dp')), may hold values from -6 to 6
- prompt_keys: bfloat16 [1024, 256], P('group'), may hold values from -6 to 6
- prompt_values: bfloat16 [1024, 256], P('group'), may hold values from -6 to 6
- norm_gain: float32 [4096], replicated, may hold values from 0.25 to 1.75
- expert_ids: int32 [2048, 8], P(('group', 'expert', 'dp')), may hold values from 0 to 15, all different within a row; in each aligned block of 64 rows (0 to 63, 64 to 127, ...) at most 42 rows name the same one
- route_weight: float32 [2048, 8], P(('group', 'expert', 'dp')), may hold values from 0.05 to 1
- stored_gate: bfloat16 [16, 4096, 768], P('expert', None, 'dp'), may hold values from -0.09375 to 0.09375
- stored_up: bfloat16 [16, 4096, 768], P('expert', None, 'dp'), may hold values from -0.09375 to 0.09375
- stored_down: bfloat16 [16, 768, 4096], P('expert', 'dp'), may hold values from -0.21875 to 0.21875
- holder: int32 [16], replicated, may hold values from 0 to 15, as said below
Outputs:
- layer_out: bfloat16 [2048, 4096], P(('group', 'expert', 'dp'))
The draws below stay inside these ranges and needn't reach their ends.
Inputs may be any that keep to these rules, and one draw needn't show every extreme that they name: `expert_ids`: each row names 8 different experts. In the 64 rows of one device no expert is named more than 42 times, and in every draw some expert is named exactly 42 times in some device's rows. holder[s] is s or the slot 8 away (s + 16 / 2 modulo 16), holder[holder[s]] = s, and holder[0] = 8.
All inputs are finite; a program needn't handle non-finite values.
Results may differ from the reference program's by a relative error of at most 0.0055.
Values may be sent and summed in bfloat16 or wider, within the bound.
A program may use at most 192 MiB of HBM per device.

```python
import math
import jax
import jax.numpy as jnp
import numpy as np
from jax import lax

D = 4096
FFW = 768
HEADS = 32
KVH = 2
HD = 128
TOPK = 8
PREFIX = 1024
TOK_DEV = 64
EXPERTS = 16
SPLITS = 2
CAP = 42
TOKENS = 2048


def drawn_keys(key):
    base = jax.random.fold_in(key, 11)
    key_width = KVH * HD
    drawn = jnp.clip(jax.random.normal(jax.random.fold_in(base, 3), (PREFIX, key_width), jnp.float32), -5.5, 5.5)
    return drawn


def draw_prompt_keys(key, part):
    drawn = drawn_keys(key)
    return drawn.astype(jnp.bfloat16)


def draw_queries(key, part):
    base = jax.random.fold_in(key, 23)
    values = jnp.clip(jax.random.normal(base, (TOKENS, HEADS * HD), jnp.float32), -5.5, 5.5)
    return values.astype(jnp.bfloat16)


def draw_holder(key, part):
    half_count = EXPERTS // 2
    flags = jax.random.randint(jax.random.fold_in(key, 3), (half_count,), 0, 2)
    flags = flags.at[0].set(1)
    lower_half = jnp.arange(half_count) + flags * half_count
    upper_half = jnp.arange(half_count) + half_count - flags * half_count
    return jnp.concatenate([lower_half, upper_half]).astype(jnp.int32)


def steps_of(stream_key, dims, shards, smallest, top_value):
    level, own = 1.0, jax.random.fold_in(stream_key, 6)
    for dim, parts in shards:
        steps = jnp.exp(jax.random.uniform(jax.random.fold_in(own, dim), (parts,), jnp.float32, smallest / len(shards), top_value / len(shards)))
        level = level * jnp.repeat(steps, dims[dim] // parts).reshape([-1 if axis == dim else 1 for axis in range(len(dims))])
    return level


def routed_block(key, own, number, rows, number_of, top, most, skew):
    order = jax.random.permutation(key, number_of)
    packed, usual = load_shares(number_of, rows * top, most, skew, True), load_shares(number_of, rows * top, most, skew, False)
    places = jnp.arange(number_of)

    def named(sizes, rotation):
        used = int((sizes > 0).sum())
        fixed = max(1, used // 4)
        passed = fixed + (places - fixed + rotation * (used - fixed)) % max(1, number_of - fixed)
        return jnp.zeros((number_of,), jnp.int32).at[order[jnp.where(places < fixed, places, passed)]].set(jnp.asarray(sizes, jnp.int32))

    sizes = jnp.where(number % 4 == 0, named(packed, number // 4), named(usual, number - number // 4 - 1))
    mixed = jax.random.permutation(jax.random.fold_in(own, 3), number_of)
    giver, receiver = mixed[0:number_of // 2 * 2:2], mixed[1:number_of // 2 * 2:2]
    room = jnp.minimum(sizes[giver] - 1, most - sizes[receiver]) // 2
    room = jnp.where((giver == order[0]) | (receiver == order[0]) | (sizes[receiver] == 0), 0, jnp.maximum(room, 0))
    passed = jax.random.randint(jax.random.fold_in(own, 4), (number_of // 2,), 0, 1 << 20) % (room + 1)
    sizes = sizes.at[giver].add(-passed).at[receiver].add(passed)
    labels = jnp.searchsorted(jnp.cumsum(sizes), jnp.arange(rows * top), side="right").astype(jnp.int32)
    table = labels.reshape(top, rows).T
    table = table[jax.random.permutation(jax.random.fold_in(own, 1), rows)]
    rotation = jax.random.randint(jax.random.fold_in(own, 2), (rows, 1), 0, top)
    return jnp.take_along_axis(table, (jnp.arange(top)[None, :] + rotation) % top, axis=1)


def load_shares(number_of, total, reach, slope, full):
    portions = [(1 << 20) // math.isqrt(grade ** slope) + 1 for grade in range(1, number_of + 1)]
    largest = reach if full else min(reach, max(-(-total // number_of), total * portions[0] // sum(portions)))
    least = 1 if total - largest >= number_of - 1 else 0
    counts, surplus = [largest] + [least] * (number_of - 1), total - largest - least * (number_of - 1)
    while surplus > 0:
        movable = [i for i in range(1, number_of) if counts[i] < largest] or [i for i in range(1, number_of) if counts[i] < reach]
        whole, left = sum([portions[i] for i in movable]), surplus
        for i in movable:
            extra = min(reach - counts[i], max(1, left * portions[i] // whole), surplus)
            counts[i] = counts[i] + extra
            surplus = surplus - extra
    return np.array(counts)


def normal_values(own_key, dims, width, limit, shards=(), kind=jnp.bfloat16):
    drawn = jax.random.normal(own_key, dims, jnp.float32) * width
    if len(shards) > 0:
        drawn = steps_of(own_key, dims, shards, -0.22, 0.18) * drawn
    return jnp.clip(drawn, min=-limit, max=limit).astype(kind)


def setup_inputs(seed: int = 0, part: int = 0) -> dict:
    keys = jax.random.split(jax.random.key(seed), 14)
    part_splits = jax.random.split(jax.random.fold_in(keys[13], part), 14)
    tokens = normal_values(part_splits[0], (TOKENS, D), 1.0, 6.0, ((0, 32),))
    queries = draw_queries(jax.random.fold_in(jax.random.fold_in(keys[13], part), 71), part)
    keys_local = normal_values(part_splits[2], (TOKENS, KVH * HD), 1.0, 6.0, ((0, 32),))
    values_local = normal_values(part_splits[3], (TOKENS, KVH * HD), 1.0, 6.0, ((0, 32),))
    prompt_keys = draw_prompt_keys(jax.random.fold_in(jax.random.fold_in(keys[13], part), 71), part)
    prompt_values = normal_values(part_splits[5], (PREFIX, KVH * HD), 1.0, 6.0)
    norm_gain = jnp.clip(1.0 + 0.15 * jax.random.normal(keys[6], (D,), jnp.float32), 0.25, 1.75)
    expert_ids_keys = jax.random.split(jax.random.fold_in(part_splits[7], 1), TOKENS // TOK_DEV)
    expert_ids_turns = jax.random.permutation(jax.random.fold_in(part_splits[7], 3), TOKENS // TOK_DEV)
    expert_ids = jax.vmap(lambda own, number: routed_block(jax.random.fold_in(part_splits[7], 2), own, number, TOK_DEV, EXPERTS, TOPK, CAP, 2))(expert_ids_keys, expert_ids_turns).reshape((TOKENS, TOPK))
    route_weight = jnp.clip(jnp.exp(math.log(1.0) - 2.9957323 * jax.random.uniform(part_splits[8], (TOKENS, TOPK), jnp.float32) ** steps_of(part_splits[8], (TOKENS, TOPK), ((0, 32),), -0.2, 0.2)), 0.05, 1.0)
    stored_gate = normal_values(keys[9], (EXPERTS, D, FFW), D ** -0.5, 0.09375, ((0, 16), (2, 2)))
    stored_up = normal_values(keys[10], (EXPERTS, D, FFW), D ** -0.5, 0.09375, ((0, 16), (2, 2)))
    stored_down = normal_values(keys[11], (EXPERTS, FFW, D), FFW ** -0.5, 0.21875, ((0, 16), (1, 2)))
    holder = draw_holder(jax.random.fold_in(keys[13], 71), part)
    return dict(tokens=tokens, queries=queries, keys_local=keys_local, values_local=values_local, prompt_keys=prompt_keys, prompt_values=prompt_values, norm_gain=norm_gain, expert_ids=expert_ids, route_weight=route_weight, stored_gate=stored_gate, stored_up=stored_up, stored_down=stored_down, holder=holder)


def attend_block(queries, keys_local, values_local, prompt_keys, prompt_values):
    count_rows = queries.shape[0]
    grouping = HEADS // KVH
    query_all = queries.astype(jnp.float32).reshape(count_rows, KVH, grouping, HD)
    key_all = jnp.concatenate([prompt_keys, keys_local], 0).astype(jnp.float32).reshape(-1, KVH, HD)
    value_all = jnp.concatenate([prompt_values, values_local], 0).astype(jnp.float32).reshape(-1, KVH, HD)
    scores = jnp.einsum('tkgd,skd->kgts', query_all, key_all) * HD ** (-0.5)
    column = jnp.arange(key_all.shape[0], dtype=jnp.int32)
    row_index = jnp.arange(count_rows, dtype=jnp.int32)
    allowed = (column[None, :] < PREFIX) | (column[None, :] - PREFIX <= row_index[:, None])
    scores = jnp.where(allowed[None, None], scores, -jnp.inf)
    highest = lax.optimization_barrier(jnp.max(scores, axis=-1, keepdims=True))
    expons = jnp.exp(scores - highest)
    weights = expons / lax.optimization_barrier(jnp.sum(expons, axis=-1, keepdims=True))
    weights = lax.optimization_barrier(weights.astype(jnp.bfloat16)).astype(jnp.float32)
    context = jnp.einsum('kgts,skd->tkgd', weights, value_all)
    return context.reshape(count_rows, HEADS * HD)

def reference(tokens, queries, keys_local, values_local, prompt_keys, prompt_values, norm_gain, expert_ids, route_weight, stored_gate, stored_up, stored_down, holder):
    block_count = TOKENS // TOK_DEV

    def one_block(items):
        return attend_block(items[0], items[1], items[2], prompt_keys, prompt_values)
    context = lax.map(one_block, (queries.reshape(block_count, TOK_DEV, -1), keys_local.reshape(block_count, TOK_DEV, -1), values_local.reshape(block_count, TOK_DEV, -1)))
    context = context.reshape(TOKENS, D)
    widened = tokens.astype(jnp.float32)
    normed = (widened * lax.rsqrt(lax.optimization_barrier(jnp.mean(widened * widened, axis=-1, keepdims=True)) + 1e-06) * norm_gain.astype(jnp.float32)).astype(jnp.bfloat16)
    shares = route_weight / lax.optimization_barrier(jnp.sum(route_weight, axis=-1, keepdims=True))
    grouped_ids = expert_ids.reshape(block_count, TOK_DEV * TOPK)
    onehot = (grouped_ids[:, :, None] == jnp.arange(EXPERTS, dtype=jnp.int32)[None, None, :]).astype(jnp.int32)
    slot_of = lax.optimization_barrier(jnp.sum((jnp.cumsum(onehot, axis=1) - onehot) * onehot, axis=2)).reshape(-1).astype(jnp.int32)
    flat_ids = expert_ids.reshape(-1).astype(jnp.int32)
    assigned = jnp.arange(TOKENS * TOPK, dtype=jnp.int32)
    anchor = (assigned // (TOK_DEV * TOPK)).astype(jnp.int32)
    token_of = (assigned // TOPK).astype(jnp.int32)
    column_at = anchor * CAP + slot_of
    row_table = jnp.full((EXPERTS, block_count * CAP), TOKENS, jnp.int32).at[flat_ids, column_at].set(token_of)
    share_table = jnp.zeros((EXPERTS, block_count * CAP), jnp.float32).at[flat_ids, column_at].set(shares.reshape(-1))
    padded = jnp.concatenate([normed, jnp.zeros((1, D), jnp.bfloat16)], 0)
    unit_count = FFW // SPLITS

    def serve(carry, inputs):
        expert_id, rows_at, scaling = inputs
        source = holder[expert_id]
        picked = padded[rows_at]
        gate_w = stored_gate[source]
        up_w = stored_up[source]
        down_w = stored_down[source]
        summed = jnp.zeros((picked.shape[0], D), jnp.float32)
        for section in range(SPLITS):
            lower = section * unit_count
            gate_val = jnp.dot(picked, gate_w[:, lower:lower + unit_count], preferred_element_type=jnp.float32)
            up_val = jnp.dot(picked, up_w[:, lower:lower + unit_count], preferred_element_type=jnp.float32)
            hidden = (jax.nn.silu(gate_val) * up_val).astype(jnp.bfloat16)
            partial_out = jnp.dot(hidden, down_w[lower:lower + unit_count], preferred_element_type=jnp.float32)
            summed = summed + lax.optimization_barrier(partial_out.astype(jnp.bfloat16)).astype(jnp.float32)
        result = lax.optimization_barrier(summed.astype(jnp.bfloat16)).astype(jnp.float32)
        carry = carry.at[rows_at].add(scaling[:, None] * result, mode='drop')
        return (carry, None)
    mixture, _ = lax.scan(serve, jnp.zeros((TOKENS, D), jnp.float32), (jnp.arange(EXPERTS, dtype=jnp.int32), row_table, share_table))
    return (widened + context + mixture).astype(jnp.bfloat16)
```

```python
import functools

import jax
import jax.numpy as jnp
from jax import lax
from jax.experimental import pallas as pl
from jax.experimental.pallas import tpu as pltpu
from jax.sharding import PartitionSpec as P

HEADS = 32
KVH = 2
HD = 128
TOPK = 8
EXP_DEV = 1
PREFIX = 1024
PAIR = 2
MESH = pl.DeviceIdType.MESH


def attend_rows(queries, keys_local, values_local, prompt_keys, prompt_values):
    count_rows = queries.shape[0]
    grouping = HEADS // KVH
    query_all = queries.reshape(count_rows, KVH, grouping, HD)
    key_all = jnp.concatenate([prompt_keys, keys_local], 0).reshape(-1, KVH, HD)
    value_all = jnp.concatenate([prompt_values, values_local], 0).reshape(-1, KVH, HD)
    scores = jnp.einsum(
        "tkgd,skd->kgts", query_all, key_all, preferred_element_type=jnp.float32
    ) * HD ** (-0.5)
    column = jnp.arange(key_all.shape[0], dtype=jnp.int32)
    row_index = jnp.arange(count_rows, dtype=jnp.int32)
    allowed = (column[None, :] < PREFIX) | (column[None, :] - PREFIX <= row_index[:, None])
    scores = jnp.where(allowed[None, None], scores, -jnp.inf)
    highest = jnp.max(scores, axis=-1, keepdims=True)
    expons = jnp.exp(scores - highest)
    weights = (expons / jnp.sum(expons, axis=-1, keepdims=True)).astype(jnp.bfloat16)
    context = jnp.einsum("kgts,skd->tkgd", weights, value_all, preferred_element_type=jnp.float32)
    return context.reshape(count_rows, HEADS * HD)


def expert_rows(picked, gate_w, up_w, down_w):
    gate_val = jnp.dot(picked, gate_w, preferred_element_type=jnp.float32)
    up_val = jnp.dot(picked, up_w, preferred_element_type=jnp.float32)
    hidden = (jax.nn.silu(gate_val) * up_val).astype(jnp.bfloat16)
    return jnp.dot(hidden, down_w, preferred_element_type=jnp.float32).astype(jnp.bfloat16)


def rows_of(place, count):
    return pl.ds(place * count, count)


def layer_body(
    slots,
    chunks,
    room,
    tok_ref,
    query_ref,
    key_ref,
    value_ref,
    pkey_ref,
    pvalue_ref,
    gain_ref,
    ids_ref,
    weight_ref,
    holder_ref,
    gate_hbm,
    up_hbm,
    down_hbm,
    out_ref,
    line_own,
    line_pair,
    packed,
    mine_rows,
    leaf_rows,
    mine_res,
    leaf_res,
    back_res,
    pair_sum,
    pair_got,
    line_sum,
    line_got,
    proj_w,
    down_w,
    mine_acc,
    leaf_acc,
    mine_hid,
    leaf_hid,
    context,
    table_own,
    table_pair,
    chooser,
    spread,
    line_send,
    line_recv,
    pair_send,
    pair_recv,
    leaf_send,
    leaf_recv,
    back_send,
    back_recv,
    sum_send,
    sum_recv,
    end_send,
    end_recv,
    table_send,
    table_recv,
    load_sem,
    give_send,
    give_recv,
):
    tok = tok_ref.shape[0]
    span = tok_ref.shape[1] // chunks
    unit = gate_hbm.shape[2]
    full = slots * tok
    plane = PAIR * PAIR
    me, core = lax.axis_index("expert"), lax.axis_index("dp")
    level, spot = me // plane, lax.rem(me, plane)
    low = 1 - 2 * lax.rem(spot, PAIR)
    high = PAIR - 2 * PAIR * (spot // PAIR)
    pair_id = me + (1 - core) * low + core * high
    leaf_id = me + core * low + (1 - core) * high
    ahead = [lax.rem(level + k, slots) * plane + spot for k in range(slots)]
    behind = [lax.rem(level + slots - k, slots) * plane + spot for k in range(slots)]

    def remote(src, dst, send, recv, expert, side=core):
        return pltpu.make_async_remote_copy(
            src_ref=src,
            dst_ref=dst,
            send_sem=send,
            recv_sem=recv,
            device_id={"expert": expert, "dp": side},
            device_id_type=MESH,
        )

    def line_copy(ch, k):
        return remote(
            line_own.at[ch, rows_of(0, tok)],
            line_own.at[ch, rows_of(k, tok)],
            line_send.at[ch, k - 1],
            line_recv.at[ch, k - 1],
            ahead[k],
        )

    def pair_copy(ch):
        return remote(line_own.at[ch], line_pair.at[ch], pair_send.at[ch], pair_recv.at[ch], pair_id)

    def leaf_copy(ch, g):
        return remote(
            packed.at[ch, rows_of(g, room)],
            leaf_rows.at[ch, rows_of(g, room)],
            leaf_send.at[ch, g],
            leaf_recv.at[ch, g],
            leaf_id,
        )

    def back_copy(ch, g):
        return remote(
            leaf_res.at[ch, rows_of(g, room)],
            back_res.at[ch, rows_of(g, room)],
            back_send.at[ch, g],
            back_recv.at[ch, g],
            leaf_id,
        )

    def sum_copy(ch):
        return remote(pair_sum.at[ch], pair_got.at[ch], sum_send.at[ch], sum_recv.at[ch], pair_id)

    def end_copy(ch, k):
        return remote(
            line_sum.at[ch, rows_of(k, tok)],
            line_got.at[ch, rows_of(k - 1, tok)],
            end_send.at[ch, k - 1],
            end_recv.at[ch, k - 1],
            behind[k],
        )

    def table_line(k):
        return remote(
            table_own.at[rows_of(0, tok)],
            table_own.at[rows_of(k, tok)],
            table_send.at[k],
            table_recv.at[k],
            ahead[k],
        )

    def table_across():
        return remote(table_own, table_pair, table_send.at[0], table_recv.at[0], pair_id)

    def weight_parts():
        return (
            (gate_hbm.at[0], lambda p: proj_w.at[:, pl.ds(p * unit, unit)]),
            (up_hbm.at[0], lambda p: proj_w.at[:, pl.ds((2 + p) * unit, unit)]),
            (down_hbm.at[0], lambda p: down_w.at[rows_of(p, unit)]),
        )

    def load(n):
        src, dst = weight_parts()[n]
        return pltpu.make_async_copy(src, dst(0), load_sem.at[n])

    def give(n):
        src, dst = weight_parts()[n]
        return remote(src, dst(1), give_send.at[n], give_recv.at[n], me, 1 - core)

    for n in range(3):
        load(n).start()

    barrier = pltpu.get_barrier_semaphore()
    for k in range(1, slots):
        pl.semaphore_signal(barrier, inc=1, device_id={"expert": ahead[k], "dp": core}, device_id_type=MESH)
    for expert, side in ((pair_id, core), (leaf_id, core), (me, 1 - core)):
        pl.semaphore_signal(barrier, inc=1, device_id={"expert": expert, "dp": side}, device_id_type=MESH)

    lanes = lax.broadcasted_iota(jnp.int32, table_pair.shape[:0] + (tok, table_pair.shape[1]), 1)
    raw = weight_ref[...]
    share = raw / jnp.sum(raw, axis=-1, keepdims=True)
    named = ids_ref[...]
    entry = jnp.zeros(lanes.shape, jnp.float32)
    for k in range(TOPK):
        entry = entry + jnp.where(lanes == named[:, k : k + 1], share[:, k : k + 1], 0.0)
    table_own[pl.ds(0, tok), :] = entry.astype(jnp.bfloat16)

    widened = tok_ref[...].astype(jnp.float32)
    inverse = lax.rsqrt(jnp.mean(widened * widened, axis=-1, keepdims=True) + 1e-06)
    for ch in range(chunks):
        cols = pl.ds(ch * span, span)
        line_own[ch, pl.ds(0, tok), :] = (
            tok_ref[:, cols].astype(jnp.float32) * inverse * gain_ref[:, cols]
        ).astype(jnp.bfloat16)

    pl.semaphore_wait(barrier, slots - 1 + 3)

    for k in range(1, slots):
        table_line(k).start()

    def send_line(ch, carry):
        for k in range(1, slots):
            line_copy(ch, k).start()
        return carry

    lax.fori_loop(0, chunks, send_line, 0)
    for n in range(3):
        give(n).start()

    def choose(table, expert, place):
        sel = (
            lax.broadcasted_iota(jnp.int32, (table.shape[1], full), 0) == expert
        ).astype(jnp.float32).astype(jnp.bfloat16)
        portion = jnp.dot(table[...], sel, preferred_element_type=jnp.float32)
        taken = portion > 0.0
        row = lax.broadcasted_iota(jnp.int32, (full, full), 0)
        col = lax.broadcasted_iota(jnp.int32, (full, full), 1)
        before = (col < row).astype(jnp.float32).astype(jnp.bfloat16)
        rank = jnp.dot(
            before, taken.astype(jnp.float32).astype(jnp.bfloat16), preferred_element_type=jnp.float32
        )
        hit = taken & (rank == col.astype(jnp.float32))
        spread[place] = jnp.where(hit, portion, 0.0)[:, :room].astype(jnp.bfloat16)
        chooser[place] = jnp.where(hit, 1.0, 0.0).T[:room].astype(jnp.bfloat16)

    my_expert, leaf_expert = holder_ref[me], holder_ref[leaf_id]

    for k in range(1, slots):
        table_line(k).wait_recv()
    table_across().start()
    choose(table_own, leaf_expert, 1)
    choose(table_own, my_expert, 0)

    group = HEADS // KVH
    heads = span // HD
    late = (
        lax.broadcasted_iota(jnp.int32, (heads * tok, tok), 1)
        > lax.rem(lax.broadcasted_iota(jnp.int32, (heads * tok, tok), 0), tok)
    )

    def attend(ch):
        asked = jnp.concatenate(
            [query_ref[:, pl.ds(pl.multiple_of(ch * span + h * HD, HD), HD)] for h in range(heads)], axis=0
        )
        cols = pl.ds(pl.multiple_of((ch * heads) // group * HD, HD), HD)
        over = (((1,), (1,)), ((), ()))
        first = lax.dot_general(asked, pkey_ref[:, cols], over, preferred_element_type=jnp.float32)
        second = lax.dot_general(asked, key_ref[:, cols], over, preferred_element_type=jnp.float32)
        first = first * HD ** (-0.5)
        second = jnp.where(late, -jnp.inf, second * HD ** (-0.5))
        peak = jnp.maximum(
            jnp.max(first, axis=-1, keepdims=True), jnp.max(second, axis=-1, keepdims=True)
        )
        first, second = jnp.exp(first - peak), jnp.exp(second - peak)
        total = jnp.sum(first, axis=-1, keepdims=True) + jnp.sum(second, axis=-1, keepdims=True)
        scale = 1.0 / total
        found = jnp.dot(
            (first * scale).astype(jnp.bfloat16), pvalue_ref[:, cols], preferred_element_type=jnp.float32
        ) + jnp.dot(
            (second * scale).astype(jnp.bfloat16), value_ref[:, cols], preferred_element_type=jnp.float32
        )
        for h in range(heads):
            context[ch, :, pl.ds(h * HD, HD)] = found[h * tok : (h + 1) * tok]

    def pick(place, rows):
        return jnp.dot(chooser[place], rows, preferred_element_type=jnp.float32).astype(jnp.bfloat16)

    def project(acc, rows, ch):
        part = jnp.dot(
            rows, proj_w[pl.ds(pl.multiple_of(ch * span, span), span), :], preferred_element_type=jnp.float32
        )

        @pl.when(ch == 0)
        def _():
            acc[...] = part

        @pl.when(ch > 0)
        def _():
            acc[...] += part

    def activate(acc, hid):
        gate = acc[:, : 2 * unit]
        hid[...] = (gate / (1.0 + jnp.exp(-gate)) * acc[:, 2 * unit :]).astype(jnp.bfloat16)

    def gather(i, carry):
        @pl.when(i < chunks)
        def _():
            for k in range(1, slots):
                line_copy(i, k).wait_recv()
            pair_copy(i).start()
            packed[i, pl.ds(0, room), :] = pick(1, line_own[i])
            mine_rows[i, pl.ds(0, room), :] = pick(0, line_own[i])
            leaf_copy(i, 0).start()
            attend(i)

        @pl.when(i == 1)
        def _():
            table_across().wait_recv()
            choose(table_pair, leaf_expert, 3)
            choose(table_pair, my_expert, 2)
            for n in range(3):
                load(n).wait()
                give(n).wait_recv()

        @pl.when((i >= 1) & (i <= chunks))
        def _():
            j = i - 1
            pair_copy(j).wait_recv()
            packed[j, pl.ds(room, room), :] = pick(3, line_pair[j])
            mine_rows[j, pl.ds(room, room), :] = pick(2, line_pair[j])
            leaf_copy(j, 1).start()
            project(mine_acc, mine_rows[j], j)

        @pl.when(i == chunks + 1)
        def _():
            activate(mine_acc, mine_hid)

        @pl.when(i >= 2)
        def _():
            j = i - 2
            for g in range(2):
                leaf_copy(j, g).wait_recv()
            project(leaf_acc, leaf_rows[j], j)

        return carry

    lax.fori_loop(0, chunks + 2, gather, 0)
    activate(leaf_acc, leaf_hid)

    def shrink(hid, ch):
        return jnp.dot(
            hid[...],
            down_w[:, pl.ds(pl.multiple_of(ch * span, span), span)],
            preferred_element_type=jnp.float32,
        ).astype(jnp.bfloat16)

    def leaf_down(ch, carry):
        leaf_res[ch] = shrink(leaf_hid, ch)
        back_copy(ch, 1).start()
        back_copy(ch, 0).start()
        return carry

    def mine_down(ch, carry):
        mine_res[ch] = shrink(mine_hid, ch)
        return carry

    lax.fori_loop(0, chunks, leaf_down, 0)
    lax.fori_loop(0, chunks, mine_down, 0)

    def merged(ch, g):
        rows = pl.ds(g * room, room)
        return jnp.dot(
            spread[2 * g], mine_res[ch, rows, :], preferred_element_type=jnp.float32
        ) + jnp.dot(spread[2 * g + 1], back_res[ch, rows, :], preferred_element_type=jnp.float32)

    def reduce(i, carry):
        @pl.when(i < chunks)
        def _():
            back_copy(i, 1).wait_recv()
            pair_sum[i] = merged(i, 1).astype(jnp.bfloat16)
            sum_copy(i).start()

        @pl.when((i >= 1) & (i <= chunks))
        def _():
            j = i - 1
            back_copy(j, 0).wait_recv()
            half = merged(j, 0)
            sum_copy(j).wait_recv()
            line_sum[j] = (half + pair_got[j].astype(jnp.float32)).astype(jnp.bfloat16)
            for k in range(1, slots):
                end_copy(j, k).start()

        @pl.when(i >= 2)
        def _():
            j = i - 2
            cols = pl.ds(pl.multiple_of(j * span, span), span)
            total = tok_ref[:, cols].astype(jnp.float32) + context[j]
            mixture = line_sum[j, pl.ds(0, tok), :].astype(jnp.float32)
            for k in range(1, slots):
                end_copy(j, k).wait_recv()
                mixture = mixture + line_got[j, rows_of(k - 1, tok), :].astype(jnp.float32)
            out_ref[:, cols] = (total + mixture).astype(jnp.bfloat16)

        return carry

    lax.fori_loop(0, chunks + 2, reduce, 0)

    def finish(ch, carry):
        for k in range(1, slots):
            line_copy(ch, k).wait_send()
            end_copy(ch, k).wait_send()
        for g in range(2):
            leaf_copy(ch, g).wait_send()
            back_copy(ch, g).wait_send()
        pair_copy(ch).wait_send()
        sum_copy(ch).wait_send()
        return carry

    lax.fori_loop(0, chunks, finish, 0)
    table_across().wait_send()
    for k in range(1, slots):
        table_line(k).wait_send()
    for n in range(3):
        give(n).wait_send()


def fused_layer(
    capacity,
    tokens,
    queries,
    keys_local,
    values_local,
    prompt_keys,
    prompt_values,
    norm_gain,
    expert_ids,
    route_weight,
    stored_gate,
    stored_up,
    stored_down,
    holder,
):
    tok, width = tokens.shape
    owners = lax.axis_size("expert")
    slots = owners // (PAIR * PAIR)
    unit = stored_gate.shape[2]
    chunks = 8
    span = width // chunks
    full = slots * tok
    room = -(-slots * capacity // 16) * 16
    bf16, f32 = jnp.bfloat16, jnp.float32
    lanes = -(-owners // 128) * 128
    vmem, hbm = pl.BlockSpec(memory_space=pltpu.VMEM), pl.BlockSpec(memory_space=pl.ANY)
    dma = pltpu.SemaphoreType.DMA
    return pl.pallas_call(
        functools.partial(layer_body, slots, chunks, room),
        out_shape=jax.ShapeDtypeStruct((tok, width), bf16),
        in_specs=[vmem] * 9 + [pl.BlockSpec(memory_space=pltpu.SMEM)] + [hbm] * 3,
        out_specs=vmem,
        scratch_shapes=[
            pltpu.VMEM((chunks, full, span), bf16),
            pltpu.VMEM((chunks, full, span), bf16),
            pltpu.VMEM((chunks, 2 * room, span), bf16),
            pltpu.VMEM((chunks, 2 * room, span), bf16),
            pltpu.VMEM((chunks, 2 * room, span), bf16),
            pltpu.VMEM((chunks, 2 * room, span), bf16),
            pltpu.VMEM((chunks, 2 * room, span), bf16),
            pltpu.VMEM((chunks, 2 * room, span), bf16),
            pltpu.VMEM((chunks, full, span), bf16),
            pltpu.VMEM((chunks, full, span), bf16),
            pltpu.VMEM((chunks, full, span), bf16),
            pltpu.VMEM((chunks, (slots - 1) * tok, span), bf16),
            pltpu.VMEM((width, 4 * unit), bf16),
            pltpu.VMEM((2 * unit, width), bf16),
            pltpu.VMEM((2 * room, 4 * unit), f32),
            pltpu.VMEM((2 * room, 4 * unit), f32),
            pltpu.VMEM((2 * room, 2 * unit), bf16),
            pltpu.VMEM((2 * room, 2 * unit), bf16),
            pltpu.VMEM((chunks, tok, span), f32),
            pltpu.VMEM((full, lanes), bf16),
            pltpu.VMEM((full, lanes), bf16),
            pltpu.VMEM((4, room, full), bf16),
            pltpu.VMEM((4, full, room), bf16),
            dma((chunks, slots - 1)),
            dma((chunks, slots - 1)),
            dma((chunks,)),
            dma((chunks,)),
            dma((chunks, 2)),
            dma((chunks, 2)),
            dma((chunks, 2)),
            dma((chunks, 2)),
            dma((chunks,)),
            dma((chunks,)),
            dma((chunks, slots - 1)),
            dma((chunks, slots - 1)),
            dma((slots,)),
            dma((slots,)),
            dma((3,)),
            dma((3,)),
            dma((3,)),
        ],
        compiler_params=pltpu.CompilerParams(
            collective_id=0, has_side_effects=True, vmem_limit_bytes=63 * 1024 * 1024
        ),
    )(
        tokens,
        queries,
        keys_local,
        values_local,
        prompt_keys,
        prompt_values,
        norm_gain.reshape(1, width),
        expert_ids,
        route_weight,
        holder,
        stored_gate,
        stored_up,
        stored_down,
    )


def local(
    tokens,
    queries,
    keys_local,
    values_local,
    prompt_keys,
    prompt_values,
    norm_gain,
    expert_ids,
    route_weight,
    stored_gate,
    stored_up,
    stored_down,
    holder,
):
    owners = lax.axis_size("expert")
    tok_count = tokens.shape[0]
    model_width = tokens.shape[1]
    capacity = min(tok_count, max(2, tok_count * TOPK * 4 // (3 * owners * EXP_DEV)))
    gate_w = stored_gate[0]
    up_w = stored_up[0]
    down_w = stored_down[0]
    cores = lax.axis_size("dp")
    devices = owners * cores
    if devices * tok_count <= 2 * cores * owners * capacity and owners % (PAIR * PAIR) == 0 and cores == 2:
        return fused_layer(
            capacity,
            tokens,
            queries,
            keys_local,
            values_local,
            prompt_keys,
            prompt_values,
            norm_gain,
            expert_ids,
            route_weight,
            stored_gate,
            stored_up,
            stored_down,
            holder,
        )
    context = attend_rows(queries, keys_local, values_local, prompt_keys, prompt_values)
    widened = tokens.astype(jnp.float32)
    normed = (
        widened * lax.rsqrt(jnp.mean(widened * widened, axis=-1, keepdims=True) + 1e-06) * norm_gain
    ).astype(jnp.bfloat16)
    shares = route_weight / jnp.sum(route_weight, axis=-1, keepdims=True)
    flat_ids = expert_ids.reshape(-1)
    onehot = (flat_ids[:, None] == jnp.arange(owners, dtype=jnp.int32)[None, :]).astype(jnp.int32)
    earlier = jnp.cumsum(onehot, axis=0) - onehot
    slot_of = jnp.sum(earlier * onehot, axis=1)
    places = (holder[flat_ids] * capacity + slot_of).reshape(tok_count, TOPK)
    chooser = (
        (jnp.arange(owners * capacity, dtype=jnp.int32)[:, None, None] == places[None])
        .any(axis=2)
        .astype(jnp.bfloat16)
    )
    send_rows = (
        jnp.dot(chooser, normed, preferred_element_type=jnp.float32)
        .astype(jnp.bfloat16)
        .reshape(owners, capacity, model_width)
    )
    both_rows = lax.all_gather(
        lax.all_to_all(send_rows, "expert", split_axis=0, concat_axis=0, tiled=True)[None],
        "dp",
        axis=0,
        tiled=True,
    )
    partial_out = expert_rows(both_rows.reshape(-1, model_width), gate_w, up_w, down_w)
    partial_out = partial_out.astype(jnp.float32).reshape(both_rows.shape)
    own_sum = lax.psum_scatter(
        partial_out.astype(jnp.bfloat16), "dp", scatter_dimension=0, tiled=True
    ).astype(jnp.float32)[0]
    results = lax.all_to_all(
        own_sum.astype(jnp.bfloat16), "expert", split_axis=0, concat_axis=0, tiled=True
    )
    gathered = results.reshape(owners * capacity, model_width)[places]
    mixture = jnp.einsum("tk,tkd->td", shares, gathered.astype(jnp.float32))
    return (widened + context + mixture).astype(jnp.bfloat16)


def solution(mesh):
    return jax.shard_map(
        local,
        mesh=mesh,
        in_specs=(
            P(("group", "expert", "dp"), None),
            P(("group", "expert", "dp"), None),
            P(("group", "expert", "dp"), None),
            P(("group", "expert", "dp"), None),
            P("group", None),
            P("group", None),
            P(),
            P(("group", "expert", "dp"), None),
            P(("group", "expert", "dp"), None),
            P("expert", None, "dp"),
            P("expert", None, "dp"),
            P("expert", "dp", None),
            P(),
        ),
        out_specs=P(("group", "expert", "dp"), None),
        check_vma=False,
    )
```

```python
import functools

import jax
import jax.numpy as jnp
from jax import lax
from jax.experimental import pallas as pl
from jax.experimental.pallas import tpu as pltpu
from jax.sharding import PartitionSpec as P

HEADS = 32
KVH = 2
HD = 128
TOPK = 8
EXP_DEV = 1
PREFIX = 1024
PAIR = 2
MESH = pl.DeviceIdType.MESH


def attend_rows(queries, keys_local, values_local, prompt_keys, prompt_values):
    count_rows = queries.shape[0]
    grouping = HEADS // KVH
    query_all = queries.reshape(count_rows, KVH, grouping, HD)
    key_all = jnp.concatenate([prompt_keys, keys_local], 0).reshape(-1, KVH, HD)
    value_all = jnp.concatenate([prompt_values, values_local], 0).reshape(-1, KVH, HD)
    scores = jnp.einsum(
        "tkgd,skd->kgts", query_all, key_all, preferred_element_type=jnp.float32
    ) * HD ** (-0.5)
    column = jnp.arange(key_all.shape[0], dtype=jnp.int32)
    row_index = jnp.arange(count_rows, dtype=jnp.int32)
    allowed = (column[None, :] < PREFIX) | (column[None, :] - PREFIX <= row_index[:, None])
    scores = jnp.where(allowed[None, None], scores, -jnp.inf)
    highest = jnp.max(scores, axis=-1, keepdims=True)
    expons = jnp.exp(scores - highest)
    weights = (expons / jnp.sum(expons, axis=-1, keepdims=True)).astype(jnp.bfloat16)
    context = jnp.einsum("kgts,skd->tkgd", weights, value_all, preferred_element_type=jnp.float32)
    return context.reshape(count_rows, HEADS * HD)


def expert_rows(picked, gate_w, up_w, down_w):
    gate_val = jnp.dot(picked, gate_w, preferred_element_type=jnp.float32)
    up_val = jnp.dot(picked, up_w, preferred_element_type=jnp.float32)
    hidden = (jax.nn.silu(gate_val) * up_val).astype(jnp.bfloat16)
    return jnp.dot(hidden, down_w, preferred_element_type=jnp.float32).astype(jnp.bfloat16)


def rows_of(place, count):
    return pl.ds(place * count, count)


def layer_body(
    slots,
    chunks,
    room,
    tok_ref,
    query_ref,
    key_ref,
    value_ref,
    pkey_ref,
    pvalue_ref,
    gain_ref,
    ids_ref,
    weight_ref,
    holder_ref,
    gate_hbm,
    up_hbm,
    down_hbm,
    out_ref,
    line_own,
    line_pair,
    packed,
    mine_rows,
    leaf_rows,
    mine_res,
    leaf_res,
    back_res,
    pair_sum,
    pair_got,
    line_sum,
    line_got,
    proj_w,
    down_w,
    mine_acc,
    leaf_acc,
    mine_hid,
    leaf_hid,
    context,
    table_own,
    table_pair,
    chooser,
    spread,
    up_send,
    down_send,
    line_recv,
    pair_send,
    pair_recv,
    leaf_send,
    leaf_recv,
    back_send,
    back_recv,
    sum_send,
    sum_recv,
    end_send,
    end_recv,
    table_send,
    table_recv,
    load_sem,
    give_send,
    give_recv,
):
    tok = tok_ref.shape[0]
    span = tok_ref.shape[1] // chunks
    unit = gate_hbm.shape[2]
    full = slots * tok
    plane = PAIR * PAIR
    me, core = lax.axis_index("expert"), lax.axis_index("dp")
    level, spot = me // plane, lax.rem(me, plane)
    low = 1 - 2 * lax.rem(spot, PAIR)
    high = PAIR - 2 * PAIR * (spot // PAIR)
    pair_id = me + (1 - core) * low + core * high
    leaf_id = me + core * low + (1 - core) * high
    ahead = [lax.rem(level + k, slots) * plane + spot for k in range(slots)]
    behind = [lax.rem(level + slots - k, slots) * plane + spot for k in range(slots)]

    def remote(src, dst, send, recv, expert, side=core):
        return pltpu.make_async_remote_copy(
            src_ref=src,
            dst_ref=dst,
            send_sem=send,
            recv_sem=recv,
            device_id={"expert": expert, "dp": side},
            device_id_type=MESH,
        )

    def line_copy(ch, slot, send, expert):
        part = line_own.at[ch, rows_of(slot, tok)]
        return remote(part, part, send, line_recv.at[ch, slot], expert)

    def up_copy(ch, d):
        return line_copy(ch, level - d, up_send.at[ch, d], me + plane)

    def down_copy(ch, d):
        return line_copy(ch, level + d, down_send.at[ch, d], me - plane)

    def pair_copy(ch, slot):
        return remote(
            line_own.at[ch, rows_of(slot, tok)],
            line_pair.at[ch, rows_of(slot, tok)],
            pair_send.at[ch, slot],
            pair_recv.at[ch, slot],
            pair_id,
        )

    def leaf_copy(ch, g):
        return remote(
            packed.at[ch, rows_of(g, room)],
            leaf_rows.at[ch, rows_of(g, room)],
            leaf_send.at[ch, g],
            leaf_recv.at[ch, g],
            leaf_id,
        )

    def back_copy(ch, g):
        return remote(
            leaf_res.at[ch, rows_of(g, room)],
            back_res.at[ch, rows_of(g, room)],
            back_send.at[ch, g],
            back_recv.at[ch, g],
            leaf_id,
        )

    def sum_copy(ch):
        return remote(pair_sum.at[ch], pair_got.at[ch], sum_send.at[ch], sum_recv.at[ch], pair_id)

    def end_copy(ch, k):
        return remote(
            line_sum.at[ch, rows_of(lax.rem(level + slots - k, slots), tok)],
            line_got.at[ch, rows_of(k - 1, tok)],
            end_send.at[ch, k - 1],
            end_recv.at[ch, k - 1],
            behind[k],
        )

    def table_line(k, slot):
        part = table_own.at[rows_of(slot, tok)]
        return remote(part, part, table_send.at[k], table_recv.at[k], ahead[k])

    def table_across():
        return remote(table_own, table_pair, table_send.at[0], table_recv.at[0], pair_id)

    def weight_parts():
        return (
            (gate_hbm.at[0], lambda p: proj_w.at[:, pl.ds(p * unit, unit)]),
            (up_hbm.at[0], lambda p: proj_w.at[:, pl.ds((2 + p) * unit, unit)]),
            (down_hbm.at[0], lambda p: down_w.at[rows_of(p, unit)]),
        )

    def load(n):
        src, dst = weight_parts()[n]
        return pltpu.make_async_copy(src, dst(0), load_sem.at[n])

    def give(n):
        src, dst = weight_parts()[n]
        return remote(src, dst(1), give_send.at[n], give_recv.at[n], me, 1 - core)

    for n in range(3):
        load(n).start()

    barrier = pltpu.get_barrier_semaphore()
    for k in range(1, slots):
        pl.semaphore_signal(barrier, inc=1, device_id={"expert": ahead[k], "dp": core}, device_id_type=MESH)
    for expert, side in ((pair_id, core), (leaf_id, core), (me, 1 - core)):
        pl.semaphore_signal(barrier, inc=1, device_id={"expert": expert, "dp": side}, device_id_type=MESH)

    raw = weight_ref[...]
    share = raw / jnp.sum(raw, axis=0, keepdims=True)
    named = ids_ref[...]
    place = lax.broadcasted_iota(jnp.int32, (table_own.shape[1], tok), 0)
    entry = jnp.zeros(place.shape, jnp.float32)
    for k in range(TOPK):
        entry = entry + jnp.where(place == named[k : k + 1], share[k : k + 1], 0.0)
    table_own[rows_of(level, tok), :] = entry.T.astype(jnp.bfloat16)

    widened = tok_ref[...].astype(jnp.float32)
    inverse = lax.rsqrt(jnp.mean(widened * widened, axis=-1, keepdims=True) + 1e-06)
    for ch in range(chunks):
        cols = pl.ds(ch * span, span)
        line_own[ch, rows_of(level, tok), :] = (
            tok_ref[:, cols].astype(jnp.float32) * inverse * gain_ref[:, cols]
        ).astype(jnp.bfloat16)

    pl.semaphore_wait(barrier, slots - 1 + 3)

    for k in range(1, slots):
        table_line(k, level).start()

    def pass_up(ch, d):
        @pl.when((level >= d) & (level + 1 < slots))
        def _():
            up_copy(ch, d).start()

    def pass_down(ch, d):
        @pl.when((level + d < slots) & (level >= 1))
        def _():
            down_copy(ch, d).start()

    def send_line(ch, carry):
        pass_up(ch, 0)
        pass_down(ch, 0)
        pair_copy(ch, level).start()
        return carry

    lax.fori_loop(0, chunks, send_line, 0)
    for n in range(3):
        give(n).start()

    def choose(table, expert, place):
        sel = (
            lax.broadcasted_iota(jnp.int32, (table.shape[1], full), 0) == expert
        ).astype(jnp.float32).astype(jnp.bfloat16)
        portion = jnp.dot(table[...], sel, preferred_element_type=jnp.float32)
        taken = portion > 0.0
        row = lax.broadcasted_iota(jnp.int32, (full, full), 0)
        col = lax.broadcasted_iota(jnp.int32, (full, full), 1)
        before = (col < row).astype(jnp.float32).astype(jnp.bfloat16)
        rank = jnp.dot(
            before, taken.astype(jnp.float32).astype(jnp.bfloat16), preferred_element_type=jnp.float32
        )
        hit = taken & (rank == col.astype(jnp.float32))
        spread[place] = jnp.where(hit, portion, 0.0)[:, :room].astype(jnp.bfloat16)
        chooser[place] = jnp.where(hit, 1.0, 0.0).T[:room].astype(jnp.bfloat16)

    my_expert, leaf_expert = holder_ref[me], holder_ref[leaf_id]

    for k in range(1, slots):
        table_line(k, lax.rem(level + slots - k, slots)).wait_recv()
    table_across().start()
    choose(table_own, leaf_expert, 1)
    choose(table_own, my_expert, 0)

    group = HEADS // KVH
    heads = span // HD
    late = (
        lax.broadcasted_iota(jnp.int32, (heads * tok, tok), 1)
        > lax.rem(lax.broadcasted_iota(jnp.int32, (heads * tok, tok), 0), tok)
    )

    def attend(ch):
        asked = jnp.concatenate(
            [query_ref[:, pl.ds(pl.multiple_of(ch * span + h * HD, HD), HD)] for h in range(heads)], axis=0
        )
        cols = pl.ds(pl.multiple_of((ch * heads) // group * HD, HD), HD)
        over = (((1,), (1,)), ((), ()))
        first = lax.dot_general(asked, pkey_ref[:, cols], over, preferred_element_type=jnp.float32)
        second = lax.dot_general(asked, key_ref[:, cols], over, preferred_element_type=jnp.float32)
        first = first * HD ** (-0.5)
        second = jnp.where(late, -jnp.inf, second * HD ** (-0.5))
        peak = jnp.maximum(
            jnp.max(first, axis=-1, keepdims=True), jnp.max(second, axis=-1, keepdims=True)
        )
        first, second = jnp.exp(first - peak), jnp.exp(second - peak)
        total = jnp.sum(first, axis=-1, keepdims=True) + jnp.sum(second, axis=-1, keepdims=True)
        scale = 1.0 / total
        found = jnp.dot(
            (first * scale).astype(jnp.bfloat16), pvalue_ref[:, cols], preferred_element_type=jnp.float32
        ) + jnp.dot(
            (second * scale).astype(jnp.bfloat16), value_ref[:, cols], preferred_element_type=jnp.float32
        )
        for h in range(heads):
            context[ch, :, pl.ds(h * HD, HD)] = found[h * tok : (h + 1) * tok]

    def pick(place, rows):
        return jnp.dot(chooser[place], rows, preferred_element_type=jnp.float32).astype(jnp.bfloat16)

    def project(acc, rows, ch):
        part = jnp.dot(
            rows, proj_w[pl.ds(pl.multiple_of(ch * span, span), span), :], preferred_element_type=jnp.float32
        )

        @pl.when(ch == 0)
        def _():
            acc[...] = part

        @pl.when(ch > 0)
        def _():
            acc[...] += part

    def activate(acc, hid):
        gate = acc[:, : 2 * unit]
        hid[...] = (gate / (1.0 + jnp.exp(-gate)) * acc[:, 2 * unit :]).astype(jnp.bfloat16)

    def hop(ch, d):
        @pl.when(level >= d)
        def _():
            line_copy(ch, level - d, up_send.at[ch, 0], me).wait_recv()
            pair_copy(ch, level - d).start()

        pass_up(ch, d)

        @pl.when(level + d < slots)
        def _():
            line_copy(ch, level + d, up_send.at[ch, 0], me).wait_recv()
            pair_copy(ch, level + d).start()

        pass_down(ch, d)

    def during(place, work):
        @pl.when((place >= 0) & (place < chunks))
        def _():
            work(place)

    def own_ready(ch):
        packed[ch, pl.ds(0, room), :] = pick(1, line_own[ch])
        mine_rows[ch, pl.ds(0, room), :] = pick(0, line_own[ch])
        leaf_copy(ch, 0).start()
        attend(ch)

    def pair_ready(ch):
        @pl.when(ch == 0)
        def _():
            table_across().wait_recv()
            choose(table_pair, leaf_expert, 3)
            choose(table_pair, my_expert, 2)
            for n in range(3):
                load(n).wait()
                give(n).wait_recv()

        for slot in range(slots):
            pair_copy(ch, slot).wait_recv()
        packed[ch, pl.ds(room, room), :] = pick(3, line_pair[ch])
        mine_rows[ch, pl.ds(room, room), :] = pick(2, line_pair[ch])
        leaf_copy(ch, 1).start()
        project(mine_acc, mine_rows[ch], ch)

        @pl.when(ch == chunks - 1)
        def _():
            activate(mine_acc, mine_hid)

    def leaf_ready(ch):
        for g in range(2):
            leaf_copy(ch, g).wait_recv()
        project(leaf_acc, leaf_rows[ch], ch)

    reach = slots - 1

    def gather(i, carry):
        for d in range(reach, 0, -1):
            during(i - (d - 1), lambda ch, d=d: hop(ch, d))
        during(i - (reach - 1), own_ready)
        during(i - reach, pair_ready)
        during(i - (reach + 1), leaf_ready)
        return carry

    lax.fori_loop(0, chunks + reach + 1, gather, 0)
    activate(leaf_acc, leaf_hid)

    def shrink(hid, ch):
        return jnp.dot(
            hid[...],
            down_w[:, pl.ds(pl.multiple_of(ch * span, span), span)],
            preferred_element_type=jnp.float32,
        ).astype(jnp.bfloat16)

    def leaf_down(ch, carry):
        leaf_res[ch] = shrink(leaf_hid, ch)
        back_copy(ch, 1).start()
        back_copy(ch, 0).start()
        return carry

    def mine_down(ch, carry):
        mine_res[ch] = shrink(mine_hid, ch)
        return carry

    lax.fori_loop(0, chunks, leaf_down, 0)
    lax.fori_loop(0, chunks, mine_down, 0)

    def merged(ch, g):
        rows = pl.ds(g * room, room)
        return jnp.dot(
            spread[2 * g], mine_res[ch, rows, :], preferred_element_type=jnp.float32
        ) + jnp.dot(spread[2 * g + 1], back_res[ch, rows, :], preferred_element_type=jnp.float32)

    def reduce(i, carry):
        @pl.when(i < chunks)
        def _():
            back_copy(i, 1).wait_recv()
            pair_sum[i] = merged(i, 1).astype(jnp.bfloat16)
            sum_copy(i).start()

        @pl.when((i >= 1) & (i <= chunks))
        def _():
            j = i - 1
            back_copy(j, 0).wait_recv()
            half = merged(j, 0)
            sum_copy(j).wait_recv()
            line_sum[j] = (half + pair_got[j].astype(jnp.float32)).astype(jnp.bfloat16)
            for k in range(1, slots):
                end_copy(j, k).start()

        @pl.when(i >= 2)
        def _():
            j = i - 2
            cols = pl.ds(pl.multiple_of(j * span, span), span)
            total = tok_ref[:, cols].astype(jnp.float32) + context[j]
            mixture = line_sum[j, rows_of(level, tok), :].astype(jnp.float32)
            for k in range(1, slots):
                end_copy(j, k).wait_recv()
                mixture = mixture + line_got[j, rows_of(k - 1, tok), :].astype(jnp.float32)
            out_ref[:, cols] = (total + mixture).astype(jnp.bfloat16)

        return carry

    lax.fori_loop(0, chunks + 2, reduce, 0)

    def finish(ch, carry):
        for d in range(slots - 1):

            @pl.when((level >= d) & (level + 1 < slots))
            def _(d=d):
                up_copy(ch, d).wait_send()

            @pl.when((level + d < slots) & (level >= 1))
            def _(d=d):
                down_copy(ch, d).wait_send()

        for k in range(1, slots):
            end_copy(ch, k).wait_send()
        for slot in range(slots):
            pair_copy(ch, slot).wait_send()
        for g in range(2):
            leaf_copy(ch, g).wait_send()
            back_copy(ch, g).wait_send()
        sum_copy(ch).wait_send()
        return carry

    lax.fori_loop(0, chunks, finish, 0)
    table_across().wait_send()
    for k in range(1, slots):
        table_line(k, level).wait_send()
    for n in range(3):
        give(n).wait_send()


def fused_layer(
    capacity,
    tokens,
    queries,
    keys_local,
    values_local,
    prompt_keys,
    prompt_values,
    norm_gain,
    expert_ids,
    route_weight,
    stored_gate,
    stored_up,
    stored_down,
    holder,
):
    tok, width = tokens.shape
    owners = lax.axis_size("expert")
    slots = owners // (PAIR * PAIR)
    unit = stored_gate.shape[2]
    chunks = 8
    span = width // chunks
    full = slots * tok
    room = -(-slots * capacity // 16) * 16
    bf16, f32 = jnp.bfloat16, jnp.float32
    lanes = -(-owners // 128) * 128
    vmem, hbm = pl.BlockSpec(memory_space=pltpu.VMEM), pl.BlockSpec(memory_space=pl.ANY)
    dma = pltpu.SemaphoreType.DMA
    return pl.pallas_call(
        functools.partial(layer_body, slots, chunks, room),
        out_shape=jax.ShapeDtypeStruct((tok, width), bf16),
        in_specs=[vmem] * 9 + [pl.BlockSpec(memory_space=pltpu.SMEM)] + [hbm] * 3,
        out_specs=vmem,
        scratch_shapes=[
            pltpu.VMEM((chunks, full, span), bf16),
            pltpu.VMEM((chunks, full, span), bf16),
            pltpu.VMEM((chunks, 2 * room, span), bf16),
            pltpu.VMEM((chunks, 2 * room, span), bf16),
            pltpu.VMEM((chunks, 2 * room, span), bf16),
            pltpu.VMEM((chunks, 2 * room, span), bf16),
            pltpu.VMEM((chunks, 2 * room, span), bf16),
            pltpu.VMEM((chunks, 2 * room, span), bf16),
            pltpu.VMEM((chunks, full, span), bf16),
            pltpu.VMEM((chunks, full, span), bf16),
            pltpu.VMEM((chunks, full, span), bf16),
            pltpu.VMEM((chunks, (slots - 1) * tok, span), bf16),
            pltpu.VMEM((width, 4 * unit), bf16),
            pltpu.VMEM((2 * unit, width), bf16),
            pltpu.VMEM((2 * room, 4 * unit), f32),
            pltpu.VMEM((2 * room, 4 * unit), f32),
            pltpu.VMEM((2 * room, 2 * unit), bf16),
            pltpu.VMEM((2 * room, 2 * unit), bf16),
            pltpu.VMEM((chunks, tok, span), f32),
            pltpu.VMEM((full, lanes), bf16),
            pltpu.VMEM((full, lanes), bf16),
            pltpu.VMEM((4, room, full), bf16),
            pltpu.VMEM((4, full, room), bf16),
            dma((chunks, slots - 1)),
            dma((chunks, slots - 1)),
            dma((chunks, slots)),
            dma((chunks, slots)),
            dma((chunks, slots)),
            dma((chunks, 2)),
            dma((chunks, 2)),
            dma((chunks, 2)),
            dma((chunks, 2)),
            dma((chunks,)),
            dma((chunks,)),
            dma((chunks, slots - 1)),
            dma((chunks, slots - 1)),
            dma((slots,)),
            dma((slots,)),
            dma((3,)),
            dma((3,)),
            dma((3,)),
        ],
        compiler_params=pltpu.CompilerParams(
            collective_id=0, has_side_effects=True, vmem_limit_bytes=63 * 1024 * 1024
        ),
    )(
        tokens,
        queries,
        keys_local,
        values_local,
        prompt_keys,
        prompt_values,
        norm_gain.reshape(1, width),
        expert_ids.T,
        route_weight.T,
        holder,
        stored_gate,
        stored_up,
        stored_down,
    )


def local(
    tokens,
    queries,
    keys_local,
    values_local,
    prompt_keys,
    prompt_values,
    norm_gain,
    expert_ids,
    route_weight,
    stored_gate,
    stored_up,
    stored_down,
    holder,
):
    owners = lax.axis_size("expert")
    tok_count = tokens.shape[0]
    model_width = tokens.shape[1]
    capacity = min(tok_count, max(2, tok_count * TOPK * 4 // (3 * owners * EXP_DEV)))
    gate_w = stored_gate[0]
    up_w = stored_up[0]
    down_w = stored_down[0]
    cores = lax.axis_size("dp")
    devices = owners * cores
    if devices * tok_count <= 2 * cores * owners * capacity and owners % (PAIR * PAIR) == 0 and cores == 2:
        return fused_layer(
            capacity,
            tokens,
            queries,
            keys_local,
            values_local,
            prompt_keys,
            prompt_values,
            norm_gain,
            expert_ids,
            route_weight,
            stored_gate,
            stored_up,
            stored_down,
            holder,
        )
    context = attend_rows(queries, keys_local, values_local, prompt_keys, prompt_values)
    widened = tokens.astype(jnp.float32)
    normed = (
        widened * lax.rsqrt(jnp.mean(widened * widened, axis=-1, keepdims=True) + 1e-06) * norm_gain
    ).astype(jnp.bfloat16)
    shares = route_weight / jnp.sum(route_weight, axis=-1, keepdims=True)
    flat_ids = expert_ids.reshape(-1)
    onehot = (flat_ids[:, None] == jnp.arange(owners, dtype=jnp.int32)[None, :]).astype(jnp.int32)
    earlier = jnp.cumsum(onehot, axis=0) - onehot
    slot_of = jnp.sum(earlier * onehot, axis=1)
    places = (holder[flat_ids] * capacity + slot_of).reshape(tok_count, TOPK)
    chooser = (
        (jnp.arange(owners * capacity, dtype=jnp.int32)[:, None, None] == places[None])
        .any(axis=2)
        .astype(jnp.bfloat16)
    )
    send_rows = (
        jnp.dot(chooser, normed, preferred_element_type=jnp.float32)
        .astype(jnp.bfloat16)
        .reshape(owners, capacity, model_width)
    )
    both_rows = lax.all_gather(
        lax.all_to_all(send_rows, "expert", split_axis=0, concat_axis=0, tiled=True)[None],
        "dp",
        axis=0,
        tiled=True,
    )
    partial_out = expert_rows(both_rows.reshape(-1, model_width), gate_w, up_w, down_w)
    partial_out = partial_out.astype(jnp.float32).reshape(both_rows.shape)
    own_sum = lax.psum_scatter(
        partial_out.astype(jnp.bfloat16), "dp", scatter_dimension=0, tiled=True
    ).astype(jnp.float32)[0]
    results = lax.all_to_all(
        own_sum.astype(jnp.bfloat16), "expert", split_axis=0, concat_axis=0, tiled=True
    )
    gathered = results.reshape(owners * capacity, model_width)[places]
    mixture = jnp.einsum("tk,tkd->td", shares, gathered.astype(jnp.float32))
    return (widened + context + mixture).astype(jnp.bfloat16)


def solution(mesh):
    return jax.shard_map(
        local,
        mesh=mesh,
        in_specs=(
            P(("group", "expert", "dp"), None),
            P(("group", "expert", "dp"), None),
            P(("group", "expert", "dp"), None),
            P(("group", "expert", "dp"), None),
            P("group", None),
            P("group", None),
            P(),
            P(("group", "expert", "dp"), None),
            P(("group", "expert", "dp"), None),
            P("expert", None, "dp"),
            P("expert", None, "dp"),
            P("expert", "dp", None),
            P(),
        ),
        out_specs=P(("group", "expert", "dp"), None),
        check_vma=False,
    )
```
